32 devices in a mesh: pp: 4 (over z), ep: 8 (over y, x, core).
Axes of the slice: x: 2, y: 2, z: 4, core: 2. Of those that a mesh axis runs over, the one named last changes fastest.
Arguments:
- inputs: bfloat16 [4, 128, 7168], P(None, 'ep'), may hold values from -16 to 16
- norm_gain: float32 [4, 7168], P('pp'), may hold values from 0.25 to 1.75
- router_weight: bfloat16 [4, 7168, 4], P('pp'), may hold values from -0.0625 to 0.0625
- gate_weight: bfloat16 [4, 7168, 4096], P('pp', None, 'ep'), may hold values from -0.0625 to 0.0625
- up_weight: bfloat16 [4, 7168, 4096], P('pp', None, 'ep'), may hold values from -0.0625 to 0.0625
- down_weight: bfloat16 [4, 1024, 28672], P('pp', None, 'ep'), may hold values from -0.1875 to 0.1875
- routing: int32 [4, 4, 128, 2], P('pp', None, 'ep'), may hold values from 0 to 3, all different within a row; in each aligned block of 16 rows (0 to 15, 16 to 31, ..., all dimensions but the last counted through in order) at most 10 rows name the same one
Outputs:
- final: bfloat16 [4, 128, 7168], P('pp', 'ep')
The draws below stay inside these ranges and needn't reach their ends.
Inputs may be any that keep to these rules, and one draw needn't show every extreme that they name: `routing`: each token names 2 different experts. Among the 16 tokens of one device in one micro-batch of one layer, no expert is named more than 10 times, and in some of these aligned blocks one expert is named exactly 10 times.
All inputs are finite; a program needn't handle non-finite values.
Results may differ from the reference program's by a relative error of at most 0.025.
Values may be sent and summed in bfloat16 or wider, within the bound.
A program may use at most 128 MiB of HBM per device.

```python
import math
import jax
import jax.numpy as jnp
import numpy as np
from jax import lax

D = 7168
HID = 1024
TOPK = 2
TOK_DEV = 16
EXPERTS = 4
MOST = 10
MB = 4
LAYERS = 4
TOKENS = 128
N_EP = 8


def draw_inputs(key, part):
    key_rows = jax.random.fold_in(key, 11)
    key_values = jax.random.fold_in(key, 12)
    values = jnp.clip(jax.random.normal(key_values, (MB, TOKENS, D), jnp.float32), -4.0, 4.0)
    row_scale = jnp.exp(jax.random.uniform(key_rows, (MB, TOKENS, 1), jnp.float32, math.log(0.4), math.log(4.0)))
    return (values * row_scale).astype(jnp.bfloat16)


def level_of(rng, extent, cuts, least, high):
    level, own = 1.0, jax.random.fold_in(rng, 6)
    for position, blocks in cuts:
        draws = jnp.exp(jax.random.uniform(jax.random.fold_in(own, position), (blocks,), jnp.float32, least / len(cuts), high / len(cuts)))
        level = level * jnp.repeat(draws, extent[position] // blocks).reshape([-1 if axis == position else 1 for axis in range(len(extent))])
    return level


def shared_out(own_key, own, number, rows, number_of, top, reach, lean):
    ranking = jax.random.permutation(own_key, number_of)
    heavy_load, usual = load_shares(number_of, rows * top, reach, lean, True), load_shares(number_of, rows * top, reach, lean, False)
    places = jnp.arange(number_of)

    def named(lengths, rotation):
        used = int((lengths > 0).sum())
        fixed = max(1, used // 4)
        passed = fixed + (places - fixed + rotation * (used - fixed)) % max(1, number_of - fixed)
        return jnp.zeros((number_of,), jnp.int32).at[ranking[jnp.where(places < fixed, places, passed)]].set(jnp.asarray(lengths, jnp.int32))

    lengths = jnp.where(number % 4 == 0, named(heavy_load, number // 4), named(usual, number - number // 4 - 1))
    mixed = jax.random.permutation(jax.random.fold_in(own, 3), number_of)
    giver, sink = mixed[0:number_of // 2 * 2:2], mixed[1:number_of // 2 * 2:2]
    slack = jnp.minimum(lengths[giver] - 1, reach - lengths[sink]) // 2
    slack = jnp.where((giver == ranking[0]) | (sink == ranking[0]) | (lengths[sink] == 0), 0, jnp.maximum(slack, 0))
    passed = jax.random.randint(jax.random.fold_in(own, 4), (number_of // 2,), 0, 1 << 20) % (slack + 1)
    lengths = lengths.at[giver].add(-passed).at[sink].add(passed)
    labels = jnp.searchsorted(jnp.cumsum(lengths), jnp.arange(rows * top), side="right").astype(jnp.int32)
    listing = labels.reshape(top, rows).T
    listing = listing[jax.random.permutation(jax.random.fold_in(own, 1), rows)]
    rotation = jax.random.randint(jax.random.fold_in(own, 2), (rows, 1), 0, top)
    return jnp.take_along_axis(listing, (jnp.arange(top)[None, :] + rotation) % top, axis=1)


def load_shares(amount, total, bound, skew, full):
    loads = [(1 << 20) // math.isqrt(standing ** skew) + 1 for standing in range(1, amount + 1)]
    largest = bound if full else min(bound, max(-(-total // amount), total * loads[0] // sum(loads)))
    least = 1 if total - largest >= amount - 1 else 0
    given, spare = [largest] + [least] * (amount - 1), total - largest - least * (amount - 1)
    while spare > 0:
        free = [i for i in range(1, amount) if given[i] < largest] or [i for i in range(1, amount) if given[i] < bound]
        pool, remaining = sum([loads[i] for i in free]), spare
        for i in free:
            more = min(bound - given[i], max(1, remaining * loads[i] // pool), spare)
            given[i] = given[i] + more
            spare = spare - more
    return np.array(given)


def bell_draw(own_key, dims, scale, bound, cuts=(), kind=jnp.bfloat16):
    result = jax.random.normal(own_key, dims, jnp.float32) * scale
    if len(cuts) > 0:
        result = level_of(own_key, dims, cuts, -0.22, 0.18) * result
    return jnp.clip(result, min=-bound, max=bound).astype(kind)


def setup_inputs(seed: int = 0) -> dict:
    splits = jax.random.split(jax.random.key(seed), 8)
    inputs = draw_inputs(jax.random.fold_in(splits[7], 71), 0)
    norm_gain = jnp.clip(1.0 + 0.15 * jax.random.normal(splits[1], (LAYERS, D), jnp.float32), 0.25, 1.75)
    router_weight = bell_draw(splits[2], (LAYERS, D, EXPERTS), D ** -0.5, 0.0625, ((0, 4),))
    gate_weight = bell_draw(splits[3], (LAYERS, D, EXPERTS * HID), D ** -0.5, 0.0625, ((0, 4), (2, 8)))
    up_weight = bell_draw(splits[4], (LAYERS, D, EXPERTS * HID), D ** -0.5, 0.0625, ((0, 4), (2, 8)))
    down_weight = bell_draw(splits[5], (LAYERS, HID, EXPERTS * D), HID ** -0.5, 0.1875, ((0, 4), (2, 8)))
    routing_keys = jax.random.split(jax.random.fold_in(splits[6], 1), LAYERS * MB * TOKENS // TOK_DEV)
    routing_turns = jax.random.permutation(jax.random.fold_in(splits[6], 3), LAYERS * MB * TOKENS // TOK_DEV)
    routing = jax.vmap(lambda own, number: shared_out(jax.random.fold_in(splits[6], 2), own, number, TOK_DEV, EXPERTS, TOPK, MOST, 2))(routing_keys, routing_turns).reshape((LAYERS, MB, TOKENS, TOPK))
    return {"inputs": inputs, "norm_gain": norm_gain, "router_weight": router_weight, "gate_weight": gate_weight, "up_weight": up_weight, "down_weight": down_weight, "routing": routing}


routed_scale = 2.5
norm_epsilon = 1e-06

def expert_rows(rows, gate_block, up_block, down_block):
    gate_proj = jnp.dot(rows, gate_block, preferred_element_type=jnp.float32)
    up_proj = jnp.dot(rows, up_block, preferred_element_type=jnp.float32)
    hidden = (jax.nn.silu(gate_proj) * up_proj).astype(jnp.bfloat16)
    return jnp.dot(hidden, down_block, preferred_element_type=jnp.float32).astype(jnp.bfloat16)

def moe_layer(activations, gain_row, router, gate_all, up_all, down_all, routes):
    current = activations.astype(jnp.float32)
    mean_square = lax.optimization_barrier(jnp.mean(current * current, axis=1, keepdims=True))
    normed = (current * lax.rsqrt(mean_square + norm_epsilon) * gain_row).astype(jnp.bfloat16)
    scores = jax.nn.sigmoid(jnp.dot(normed, router, preferred_element_type=jnp.float32))
    expert_ids = jnp.arange(EXPERTS, dtype=jnp.int32)
    onehot = (routes[:, :, None] == expert_ids[None, None, :]).astype(jnp.float32)
    picked = lax.optimization_barrier(jnp.sum(onehot * scores[:, None, :], axis=2))
    mixing = routed_scale * picked / lax.optimization_barrier(jnp.sum(picked, axis=1, keepdims=True))
    expert_mix = lax.optimization_barrier(jnp.sum(onehot * mixing[:, :, None], axis=1))
    chosen = lax.optimization_barrier(jnp.sum(onehot, axis=1)) > 0.5
    capacity = N_EP * MOST

    def one_expert(expert):
        column = chosen[:, expert]
        members = jnp.nonzero(column, size=capacity, fill_value=0)[0].astype(jnp.int32)
        live_count = jnp.sum(column.astype(jnp.int32))
        is_live = jnp.arange(capacity, dtype=jnp.int32) < live_count
        gate_block = lax.dynamic_slice_in_dim(gate_all, expert * HID, HID, 1)
        up_block = lax.dynamic_slice_in_dim(up_all, expert * HID, HID, 1)
        down_block = lax.dynamic_slice_in_dim(down_all, expert * D, D, 1)
        outcome = expert_rows(normed[members], gate_block, up_block, down_block)
        share_weight = jnp.where(is_live, expert_mix[members, expert], 0.0)
        return (members, share_weight[:, None] * outcome.astype(jnp.float32))
    members, contributions = lax.map(one_expert, expert_ids)
    combined = jnp.zeros((TOKENS, D), jnp.float32).at[members.reshape(-1)].add(contributions.reshape(-1, D))
    return (current + combined).astype(jnp.bfloat16)

def reference(inputs, norm_gain, router_weight, gate_weight, up_weight, down_weight, routing):

    def one_batch(batch_index):

        def one_layer(activations, layer_index):
            updated = moe_layer(activations, norm_gain[layer_index], router_weight[layer_index], gate_weight[layer_index], up_weight[layer_index], down_weight[layer_index], routing[layer_index, batch_index])
            return (updated, None)
        finished, unused = lax.scan(one_layer, inputs[batch_index], jnp.arange(LAYERS, dtype=jnp.int32))
        return finished
    return lax.map(one_batch, jnp.arange(MB, dtype=jnp.int32))
```

```python
import functools

import jax
import jax.numpy as jnp
from jax import lax
from jax.experimental import pallas as pl
from jax.experimental.pallas import tpu as pltpu
from jax.sharding import PartitionSpec as P

routed_scale = 2.5
norm_epsilon = 1e-06


def kernel(
    n_pp, n_ep, experts,
    inputs_ref, gain_ref, router_ref, gate_hbm, up_hbm, down_hbm, routing_ref,
    out_ref,
    xin, xout, fin, tokens, mixes, wg, wu, wd, acc_g, acc_u, hid_own, hid_par, partial, pair_sum,
    s_buf, r_buf, s_core, r_core,
    load_sem, weight_sem, tok_send, tok_recv, hid_send, hid_recv, red_send, red_recv,
    core_send, core_recv, x_send, x_recv, fin_send, fin_recv,
):
    section = lax.axis_index("pp")
    me = lax.axis_index("ep")
    member, chip = me % 2, me // 2
    last = n_pp - 1
    bits = n_ep.bit_length() - 1
    micro_count, rows, width = xin.shape
    half = width // 2
    quarter = half // 2
    n_chip = n_ep // 2
    all_rows = n_ep * rows
    hid = wg.shape[1]

    def at_bit(b):
        return me + (1 << b) - 2 * (1 << b) * ((me // (1 << b)) % 2)

    def flip(value, mask):
        for b in range(bits):
            if mask >> b & 1:
                value = value + (1 << b) - 2 * (1 << b) * ((value // (1 << b)) % 2)
        return value

    copies = [
        pltpu.make_async_copy(gate_hbm.at[0], wg, weight_sem.at[0]),
        pltpu.make_async_copy(up_hbm.at[0], wu, weight_sem.at[1]),
        pltpu.make_async_copy(down_hbm.at[0], wd, weight_sem.at[2]),
    ]
    load = pltpu.make_async_copy(inputs_ref, xin, load_sem)

    @pl.when(section == 0)
    def _():
        load.start()

    for copy in copies:
        copy.start()

    barrier = pltpu.get_barrier_semaphore()
    for b in range(bits):
        pl.semaphore_signal(
            barrier, inc=1, device_id={"ep": at_bit(b)}, device_id_type=pl.DeviceIdType.MESH
        )
    for step in range(1, n_pp):
        pl.semaphore_signal(
            barrier, inc=1, device_id={"pp": (section + step) % n_pp},
            device_id_type=pl.DeviceIdType.MESH,
        )
    pl.semaphore_wait(barrier, bits + n_pp - 1)

    @pl.when(section == 0)
    def _():
        load.wait()

    chip_bits = list(range(1, bits))
    gather_orders = [chip_bits + [0], chip_bits[::-1] + [0], chip_bits + [0]]

    def token_copy(stream, rel):
        order = gather_orders[stream]
        hop = [b for b in order if rel >> b & 1][-1]
        source = flip(me, rel ^ (1 << hop))
        ref = mixes.at[source] if stream == 2 else tokens.at[stream, source]
        return pltpu.make_async_remote_copy(
            src_ref=ref, dst_ref=ref,
            send_sem=tok_send.at[stream, rel], recv_sem=tok_recv.at[stream, rel],
            device_id={"ep": at_bit(hop)}, device_id_type=pl.DeviceIdType.MESH,
        )

    def token_arrival(stream, rel):
        ref = mixes.at[flip(me, rel)] if stream == 2 else tokens.at[stream, flip(me, rel)]
        pltpu.make_async_remote_copy(
            src_ref=ref, dst_ref=ref,
            send_sem=tok_send.at[stream, rel], recv_sem=tok_recv.at[stream, rel],
            device_id={"ep": at_bit(0)}, device_id_type=pl.DeviceIdType.MESH,
        ).wait_recv()

    def onward(stream, rel):
        order = gather_orders[stream]
        start = max([order.index(b) for b in range(bits) if rel >> b & 1], default=-1) + 1
        return [rel | 1 << b for b in order[start:]]

    reduce_orders = [list(range(bits - 1)), list(range(bits - 1))[::-1]]

    def first_place(part, rel):
        return min(i for i, b in enumerate(reduce_orders[part]) if rel >> b & 1)

    def reduce_copy(part, rel):
        hop = reduce_orders[part][first_place(part, rel)]
        return pltpu.make_async_remote_copy(
            src_ref=s_buf.at[part, rel - 1], dst_ref=r_buf.at[part, rel - 1],
            send_sem=red_send.at[part, rel], recv_sem=red_recv.at[part, rel],
            device_id={"ep": at_bit(hop + 1)}, device_id_type=pl.DeviceIdType.MESH,
        )

    def reduced(part, rel):
        place = len(reduce_orders[part]) if rel == 0 else first_place(part, rel)
        value = partial[part, flip(me, rel << 1) // 2]
        for b in reduce_orders[part][:place]:
            reduce_copy(part, rel | 1 << b).wait_recv()
            value = value + r_buf[part, (rel | 1 << b) - 1].astype(jnp.float32)
        return value

    def in_phase(part, place):
        found = [q for q in range(1, n_chip) if first_place(part, q) == place]
        return sorted(found, key=lambda q: -bin(q).count("1"))

    hid_copy = pltpu.make_async_remote_copy(
        src_ref=hid_own, dst_ref=hid_par, send_sem=hid_send, recv_sem=hid_recv,
        device_id={"ep": at_bit(0)}, device_id_type=pl.DeviceIdType.MESH,
    )

    def core_copy(part):
        return pltpu.make_async_remote_copy(
            src_ref=s_core.at[part], dst_ref=r_core.at[part],
            send_sem=core_send.at[part], recv_sem=core_recv.at[part],
            device_id={"ep": at_bit(0)}, device_id_type=pl.DeviceIdType.MESH,
        )

    def relay_copy(micro):
        return pltpu.make_async_remote_copy(
            src_ref=xout.at[micro], dst_ref=xin.at[micro],
            send_sem=x_send.at[micro], recv_sem=x_recv.at[micro],
            device_id={"pp": (section + 1) % n_pp}, device_id_type=pl.DeviceIdType.MESH,
        )

    def final_copy(micro):
        return pltpu.make_async_remote_copy(
            src_ref=xout.at[micro], dst_ref=fin,
            send_sem=fin_send.at[micro], recv_sem=fin_recv,
            device_id={"pp": micro}, device_id_type=pl.DeviceIdType.MESH,
        )

    def one_micro(micro, unused):
        @pl.when(section > 0)
        def _():
            relay_copy(micro).wait_recv()

        current = xin[micro].astype(jnp.float32)
        mean_square = jnp.mean(current * current, axis=1, keepdims=True)
        normed = (current * lax.rsqrt(mean_square + norm_epsilon) * gain_ref[...]).astype(
            jnp.bfloat16
        )
        tokens[0, me] = normed[:, :half]
        tokens[1, me] = normed[:, half:]
        own = [onward(stream, 0) for stream in range(2)]
        for place in range(bits):
            for stream in range(2):
                token_copy(stream, own[stream][place]).start()

        normed32 = normed.astype(jnp.float32)
        routes = routing_ref[micro]
        top = routes.shape[1]
        picked = [jnp.zeros((rows, 1), jnp.float32) for k in range(top)]
        for e in range(experts):
            logit = jnp.sum(normed32 * router_ref[e : e + 1, :], axis=1, keepdims=True)
            score = jax.nn.sigmoid(logit)
            for k in range(top):
                picked[k] = picked[k] + jnp.where(routes[:, k : k + 1] == e, score, 0.0)
        total = functools.reduce(lambda a, b: a + b, picked)
        lanes = lax.broadcasted_iota(jnp.int32, (rows, 128), 1)
        mix = jnp.zeros((rows, 128), jnp.float32)
        for k in range(top):
            share = routed_scale * picked[k] / total
            mix = mix + jnp.where(lanes == routes[:, k : k + 1], share, 0.0)
        mixes[me] = mix
        for rel in onward(2, 0):
            token_copy(2, rel).start()

        order = sorted(range(1, n_ep), key=lambda r: (bin(r >> 1).count("1"), r & 1))
        for rel in order:
            for stream in range(3):
                token_arrival(stream, rel)
                for later in onward(stream, rel):
                    token_copy(stream, later).start()

        @pl.when(micro == 0)
        def _():
            copies[0].wait()
            copies[1].wait()

        acc_g[...] = jnp.zeros_like(acc_g)
        acc_u[...] = jnp.zeros_like(acc_u)
        depth = 512
        for stream in range(2):

            def project(i, carry, stream=stream):
                at = pl.multiple_of(i * depth, depth)
                block = tokens[stream, :, :, pl.ds(at, depth)].reshape(all_rows, depth)
                where = pl.ds(pl.multiple_of(stream * half + at, depth), depth)
                acc_g[...] += jnp.dot(block, wg[where, :], preferred_element_type=jnp.float32)
                acc_u[...] += jnp.dot(block, wu[where, :], preferred_element_type=jnp.float32)
                return carry

            lax.fori_loop(0, half // depth, project, 0)
        gate_proj = acc_g[...]
        hid_own[...] = (gate_proj / (1.0 + jnp.exp(-gate_proj)) * acc_u[...]).astype(jnp.bfloat16)
        hid_copy.start()
        for rel in range(1, n_ep):
            for stream in range(3):
                token_copy(stream, rel).wait_send()

        @pl.when(micro == 0)
        def _():
            copies[2].wait()

        lane3 = lax.broadcasted_iota(jnp.int32, (n_ep, rows, 128), 2)
        mix_all = jnp.sum(
            jnp.where(lane3 == chip, mixes[...], 0.0), axis=2, keepdims=True
        ).reshape(all_rows, 1)
        hid_copy.wait()

        tile = 256
        own_rows = pl.ds(pl.multiple_of(member * hid, hid), hid)
        par_rows = pl.ds(pl.multiple_of((1 - member) * hid, hid), hid)
        for part in range(2):

            def down(i, carry, part=part):
                at = pl.ds(pl.multiple_of(part * quarter + i * tile, tile), tile)
                value = jnp.dot(hid_own[...], wd[own_rows, at], preferred_element_type=jnp.float32)
                value += jnp.dot(hid_par[...], wd[par_rows, at], preferred_element_type=jnp.float32)
                value = value * mix_all
                to = pl.ds(pl.multiple_of(i * tile, tile), tile)
                partial[part, :, :, to] = value.reshape(n_chip, 2 * rows, tile)
                return carry

            lax.fori_loop(0, quarter // tile, down, 0)
            for rel in in_phase(part, 0):
                s_buf[part, rel - 1] = reduced(part, rel).astype(jnp.bfloat16)
                reduce_copy(part, rel).start()
        for place in range(1, bits - 1):
            for part in range(2):
                for rel in in_phase(part, place):
                    s_buf[part, rel - 1] = reduced(part, rel).astype(jnp.bfloat16)
                    reduce_copy(part, rel).start()
        for part in range(2):
            pair_sum[part] = reduced(part, 0).reshape(2, rows, quarter)
            s_core[part] = pair_sum[part, 1 - member].astype(jnp.bfloat16)
            core_copy(part).start()
        for part in range(2):
            at = pl.ds(pl.multiple_of(member * half + part * quarter, 128), quarter)
            xout[micro, :, at] = (
                xin[micro, :, at].astype(jnp.float32) + pair_sum[part, member]
            ).astype(jnp.bfloat16)
        for part in range(2):
            core_copy(part).wait()
            at = pl.ds(pl.multiple_of((1 - member) * half + part * quarter, 128), quarter)
            xout[micro, :, at] = (
                xin[micro, :, at].astype(jnp.float32) + r_core[part].astype(jnp.float32)
            ).astype(jnp.bfloat16)

        @pl.when(section < last)
        def _():
            relay_copy(micro).start()

        @pl.when(jnp.logical_and(section == last, micro < last))
        def _():
            final_copy(micro).start()

        for part in range(2):
            for rel in range(1, n_chip):
                reduce_copy(part, rel).wait_send()
        return unused

    lax.fori_loop(0, micro_count, one_micro, 0)

    @pl.when(section < last)
    def _():
        for micro in range(micro_count):
            relay_copy(micro).wait_send()
        final_copy(0).wait_recv()
        out_ref[0] = fin[...]

    @pl.when(section == last)
    def _():
        for micro in range(micro_count - 1):
            final_copy(micro).wait_send()
        out_ref[0] = xout[micro_count - 1]


def on_device(inputs, norm_gain, router_weight, gate_weight, up_weight, down_weight, routing):
    n_pp, n_ep = lax.axis_size("pp"), lax.axis_size("ep")
    micro_count, rows, width = inputs.shape
    experts = router_weight.shape[2]
    hid = gate_weight.shape[2]
    half = width // 2
    quarter = half // 2
    n_chip = n_ep // 2
    router_rows = router_weight[0].T.astype(jnp.float32)
    bf16, f32 = jnp.bfloat16, jnp.float32
    dma = pltpu.SemaphoreType.DMA
    any_spec = pl.BlockSpec(memory_space=pl.ANY)
    vmem_spec = pl.BlockSpec(memory_space=pltpu.VMEM)
    return pl.pallas_call(
        functools.partial(kernel, n_pp, n_ep, experts),
        out_shape=jax.ShapeDtypeStruct((1, rows, width), bf16),
        in_specs=[any_spec, vmem_spec, vmem_spec, any_spec, any_spec, any_spec, vmem_spec],
        out_specs=vmem_spec,
        scratch_shapes=[
            pltpu.VMEM((micro_count, rows, width), bf16),
            pltpu.VMEM((micro_count, rows, width), bf16),
            pltpu.VMEM((rows, width), bf16),
            pltpu.VMEM((2, n_ep, rows, half), bf16),
            pltpu.VMEM((n_ep, rows, 128), f32),
            pltpu.VMEM((width, hid), bf16),
            pltpu.VMEM((width, hid), bf16),
            pltpu.VMEM((2 * hid, half), bf16),
            pltpu.VMEM((n_ep * rows, hid), f32),
            pltpu.VMEM((n_ep * rows, hid), f32),
            pltpu.VMEM((n_ep * rows, hid), bf16),
            pltpu.VMEM((n_ep * rows, hid), bf16),
            pltpu.VMEM((2, n_chip, 2 * rows, quarter), f32),
            pltpu.VMEM((2, 2, rows, quarter), f32),
            pltpu.VMEM((2, n_chip - 1, 2 * rows, quarter), bf16),
            pltpu.VMEM((2, n_chip - 1, 2 * rows, quarter), bf16),
            pltpu.VMEM((2, rows, quarter), bf16),
            pltpu.VMEM((2, rows, quarter), bf16),
            dma, dma((3,)), dma((3, n_ep)), dma((3, n_ep)), dma, dma,
            dma((2, n_chip)), dma((2, n_chip)), dma((2,)), dma((2,)),
            dma((micro_count,)), dma((micro_count,)), dma((micro_count,)), dma,
        ],
        compiler_params=pltpu.CompilerParams(
            collective_id=0, has_side_effects=True, vmem_limit_bytes=60 * 1024 * 1024
        ),
    )(inputs, norm_gain, router_rows, gate_weight, up_weight, down_weight, routing[0])


def solution(mesh):
    return jax.shard_map(
        on_device,
        mesh=mesh,
        in_specs=(
            P(None, "ep", None),
            P("pp", None),
            P("pp", None, None),
            P("pp", None, "ep"),
            P("pp", None, "ep"),
            P("pp", None, "ep"),
            P("pp", None, "ep", None),
        ),
        out_specs=P("pp", "ep", None),
        check_vma=False,
    )
```

```python
import functools

import jax
import jax.numpy as jnp
from jax import lax
from jax.experimental import pallas as pl
from jax.experimental.pallas import tpu as pltpu
from jax.sharding import PartitionSpec as P

routed_scale = 2.5
norm_epsilon = 1e-06


def cut(size, wanted=4, unit=256):
    units = size // unit
    shares = [units // wanted + (k < units % wanted) for k in range(wanted)]
    starts = [sum(shares[:k]) for k in range(wanted)]
    return [(start * unit, share * unit) for start, share in zip(starts, shares)]


def kernel(
    n_pp, n_ep, experts,
    inputs_ref, gain_ref, router_ref, gate_hbm, up_hbm, down_hbm, routing_ref,
    out_ref,
    xin, xout, fin, tokens, mixes, wg, wu, wd, acc_g, acc_u, squares, hid_own, hid_par, partial, pair_sum,
    s_buf, r_buf, s_core, r_core,
    load_sem, weight_sem, tok_send, tok_recv, hid_send, hid_recv, red_send, red_recv,
    core_send, core_recv, x_send, x_recv, fin_send, fin_recv,
):
    section = lax.axis_index("pp")
    me = lax.axis_index("ep")
    member, chip = me % 2, me // 2
    last = n_pp - 1
    bits = n_ep.bit_length() - 1
    micro_count, unused, rows, half = xin.shape
    width = 2 * half
    parts = cut(half)
    n_part = len(parts)
    n_chip = n_ep // 2
    all_rows = n_ep * rows
    hid = wg.shape[1]

    def at_bit(b):
        return me + (1 << b) - 2 * (1 << b) * ((me // (1 << b)) % 2)

    def flip(value, mask):
        for b in range(bits):
            if mask >> b & 1:
                value = value + (1 << b) - 2 * (1 << b) * ((value // (1 << b)) % 2)
        return value

    copies = [
        pltpu.make_async_copy(gate_hbm.at[0], wg, weight_sem.at[0]),
        pltpu.make_async_copy(up_hbm.at[0], wu, weight_sem.at[1]),
        pltpu.make_async_copy(down_hbm.at[0], wd, weight_sem.at[2]),
    ]
    loads = [
        pltpu.make_async_copy(
            inputs_ref.at[:, :, pl.ds(side * half, half)], xin.at[:, side], load_sem.at[side]
        )
        for side in range(2)
    ]

    @pl.when(section == 0)
    def _():
        for load in loads:
            load.start()

    for copy in copies:
        copy.start()

    barrier = pltpu.get_barrier_semaphore()
    for b in range(bits):
        pl.semaphore_signal(
            barrier, inc=1, device_id={"ep": at_bit(b)}, device_id_type=pl.DeviceIdType.MESH
        )
    for step in range(1, n_pp):
        pl.semaphore_signal(
            barrier, inc=1, device_id={"pp": (section + step) % n_pp},
            device_id_type=pl.DeviceIdType.MESH,
        )
    pl.semaphore_wait(barrier, bits + n_pp - 1)

    @pl.when(section == 0)
    def _():
        for load in loads:
            load.wait()

    chip_bits = list(range(1, bits))
    gather_orders = [chip_bits[:: 1 - 2 * (p % 2)] + [0] for p in range(n_part)] + [chip_bits + [0]]

    def columns(part):
        return pl.ds(parts[part][0], parts[part][1])

    def token_ref(stream, source):
        if stream == n_part:
            return mixes.at[source]
        return tokens.at[:, source, :, columns(stream)]

    def token_copy(stream, rel, micro):
        order = gather_orders[stream]
        hop = [b for b in order if rel >> b & 1][-1]
        before = rel ^ (1 << hop)
        source = flip(me, before)
        src_ref = token_ref(stream, source)
        if before == 0 and stream < n_part:
            src_ref = xin.at[micro, :, :, columns(stream)]
        return pltpu.make_async_remote_copy(
            src_ref=src_ref, dst_ref=token_ref(stream, source),
            send_sem=tok_send.at[stream, rel], recv_sem=tok_recv.at[stream, rel],
            device_id={"ep": at_bit(hop)}, device_id_type=pl.DeviceIdType.MESH,
        )

    def token_arrival(stream, rel):
        ref = token_ref(stream, flip(me, rel))
        pltpu.make_async_remote_copy(
            src_ref=ref, dst_ref=ref,
            send_sem=tok_send.at[stream, rel], recv_sem=tok_recv.at[stream, rel],
            device_id={"ep": at_bit(0)}, device_id_type=pl.DeviceIdType.MESH,
        ).wait_recv()

    def onward(stream, rel):
        order = gather_orders[stream]
        start = max([order.index(b) for b in range(bits) if rel >> b & 1], default=-1) + 1
        return [rel | 1 << b for b in order[start:]]

    reduce_orders = [list(range(bits - 1))[:: 1 - 2 * (p % 2)] for p in range(n_part)]

    def first_place(part, rel):
        return min(i for i, b in enumerate(reduce_orders[part]) if rel >> b & 1)

    def reduce_copy(part, rel):
        hop = reduce_orders[part][first_place(part, rel)]
        return pltpu.make_async_remote_copy(
            src_ref=s_buf.at[rel - 1, :, columns(part)], dst_ref=r_buf.at[rel - 1, :, columns(part)],
            send_sem=red_send.at[part, rel], recv_sem=red_recv.at[part, rel],
            device_id={"ep": at_bit(hop + 1)}, device_id_type=pl.DeviceIdType.MESH,
        )

    def reduced(part, rel):
        place = len(reduce_orders[part]) if rel == 0 else first_place(part, rel)
        value = partial[flip(me, rel << 1) // 2, :, columns(part)]
        for b in reduce_orders[part][:place]:
            reduce_copy(part, rel | 1 << b).wait_recv()
            value = value + r_buf[(rel | 1 << b) - 1, :, columns(part)].astype(jnp.float32)
        return value

    def in_phase(part, place):
        found = [q for q in range(1, n_chip) if first_place(part, q) == place]
        return sorted(found, key=lambda q: -bin(q).count("1"))

    hid_copy = pltpu.make_async_remote_copy(
        src_ref=hid_own, dst_ref=hid_par, send_sem=hid_send, recv_sem=hid_recv,
        device_id={"ep": at_bit(0)}, device_id_type=pl.DeviceIdType.MESH,
    )

    def core_copy(part):
        return pltpu.make_async_remote_copy(
            src_ref=s_core.at[:, columns(part)], dst_ref=r_core.at[:, columns(part)],
            send_sem=core_send.at[part], recv_sem=core_recv.at[part],
            device_id={"ep": at_bit(0)}, device_id_type=pl.DeviceIdType.MESH,
        )

    def relay_copy(micro, part):
        return pltpu.make_async_remote_copy(
            src_ref=xout.at[micro, :, :, columns(part)], dst_ref=xin.at[micro, :, :, columns(part)],
            send_sem=x_send.at[micro, part], recv_sem=x_recv.at[micro, part],
            device_id={"pp": (section + 1) % n_pp}, device_id_type=pl.DeviceIdType.MESH,
        )

    def final_copy(micro):
        return pltpu.make_async_remote_copy(
            src_ref=xout.at[micro], dst_ref=fin,
            send_sem=fin_send.at[micro], recv_sem=fin_recv,
            device_id={"pp": micro}, device_id_type=pl.DeviceIdType.MESH,
        )

    def one_micro(micro, unused):
        acc_g[...] = jnp.zeros_like(acc_g)
        acc_u[...] = jnp.zeros_like(acc_u)
        squares[...] = jnp.zeros_like(squares)
        tile = 256
        single = [r for r in range(1, n_ep) if r & 1 == 0 and bin(r).count("1") == 1]
        others = sorted(
            [r for r in range(1, n_ep) if r not in single],
            key=lambda r: (bin(r >> 1).count("1"), r & 1),
        )

        def arrive(stream, rels):
            for rel in rels:
                token_arrival(stream, rel)
                for later in onward(stream, rel):
                    token_copy(stream, later, micro).start()

        def project_part(part):
            start, size = parts[part]

            def project(i, carry):
                side = i // (size // tile)
                at = pl.multiple_of(start + (i - side * (size // tile)) * tile, tile)
                where = pl.ds(pl.multiple_of(side * half + at, tile), tile)
                block = tokens[side, :, :, pl.ds(at, tile)].reshape(all_rows, tile)
                block = block.astype(jnp.float32)
                square = block * block
                squares[...] += functools.reduce(
                    lambda a, b: a + b, [square[:, k : k + 128] for k in range(0, tile, 128)]
                )
                block = (block * gain_ref[:, where]).astype(jnp.bfloat16)
                acc_g[...] += jnp.dot(block, wg[where, :], preferred_element_type=jnp.float32)
                acc_u[...] += jnp.dot(block, wu[where, :], preferred_element_type=jnp.float32)
                return carry

            lax.fori_loop(0, 2 * size // tile, project, 0)

        for step in range(n_part + 2):
            if step < n_part:

                @pl.when(section > 0)
                def _():
                    relay_copy(micro, step).wait_recv()

                for rel in onward(step, 0):
                    token_copy(step, rel, micro).start()
                tokens[:, me, :, columns(step)] = xin[micro, :, :, columns(step)]
            if step == n_part - 1:
                sides = [xin[micro, side].astype(jnp.float32) for side in range(2)]
                total = sum(jnp.sum(v * v, axis=1, keepdims=True) for v in sides)
                scale = lax.rsqrt(total / width + norm_epsilon)
                normed = [
                    (sides[k] * scale * gain_ref[:, k * half : (k + 1) * half])
                    .astype(jnp.bfloat16)
                    .astype(jnp.float32)
                    for k in range(2)
                ]
                routes = routing_ref[micro]
                top = routes.shape[1]
                picked = [jnp.zeros((rows, 1), jnp.float32) for k in range(top)]
                for e in range(experts):
                    logit = sum(
                        jnp.sum(
                            normed[k] * router_ref[e : e + 1, k * half : (k + 1) * half],
                            axis=1, keepdims=True,
                        )
                        for k in range(2)
                    )
                    score = jax.nn.sigmoid(logit)
                    for k in range(top):
                        picked[k] = picked[k] + jnp.where(routes[:, k : k + 1] == e, score, 0.0)
                total = functools.reduce(lambda a, b: a + b, picked)
                lanes = lax.broadcasted_iota(jnp.int32, (rows, 128), 1)
                mix = jnp.zeros((rows, 128), jnp.float32)
                for k in range(top):
                    share = routed_scale * picked[k] / total
                    mix = mix + jnp.where(lanes == routes[:, k : k + 1], share, 0.0)
                mixes[me] = mix
                for rel in onward(n_part, 0):
                    token_copy(n_part, rel, micro).start()
            if 1 <= step <= n_part:
                arrive(step - 1, single)
            if step >= 2:
                arrive(step - 2, others)
                if step == 2:

                    @pl.when(micro == 0)
                    def _():
                        copies[0].wait()
                        copies[1].wait()

                if step == n_part + 1:
                    arrive(n_part, single + others)
                project_part(step - 2)

        scale = lax.rsqrt(
            jnp.sum(squares[...], axis=1, keepdims=True) / width + norm_epsilon
        )
        gate_proj = acc_g[...] * scale
        hid_own[...] = (
            gate_proj / (1.0 + jnp.exp(-gate_proj)) * (acc_u[...] * scale)
        ).astype(jnp.bfloat16)
        hid_copy.start()
        for rel in range(1, n_ep):
            for stream in range(n_part + 1):
                token_copy(stream, rel, micro).wait_send()

        @pl.when(micro == 0)
        def _():
            copies[2].wait()

        lane3 = lax.broadcasted_iota(jnp.int32, (n_ep, rows, 128), 2)
        mix_all = jnp.sum(
            jnp.where(lane3 == chip, mixes[...], 0.0), axis=2, keepdims=True
        ).reshape(all_rows, 1)
        hid_copy.wait()

        own_rows = pl.ds(pl.multiple_of(member * hid, hid), hid)
        par_rows = pl.ds(pl.multiple_of((1 - member) * hid, hid), hid)

        def send_reduced(part, rel):
            s_buf[rel - 1, :, columns(part)] = reduced(part, rel).astype(jnp.bfloat16)
            reduce_copy(part, rel).start()

        for part in range(n_part):

            def down(i, carry, part=part):
                at = pl.ds(pl.multiple_of(parts[part][0] + i * tile, tile), tile)
                value = jnp.dot(hid_own[...], wd[own_rows, at], preferred_element_type=jnp.float32)
                value += jnp.dot(hid_par[...], wd[par_rows, at], preferred_element_type=jnp.float32)
                value = value * mix_all
                partial[:, :, at] = value.reshape(n_chip, 2 * rows, tile)
                return carry

            lax.fori_loop(0, parts[part][1] // tile, down, 0)
            for rel in in_phase(part, 0):
                send_reduced(part, rel)
        for step in range(n_part + 2):
            if step < n_part:
                for place in range(1, bits - 1):
                    for rel in in_phase(step, place):
                        send_reduced(step, rel)
            if 1 <= step <= n_part:
                part = step - 1
                at = columns(part)
                pair_sum[:, :, at] = reduced(part, 0).reshape(2, rows, parts[part][1])
                s_core[:, at] = pair_sum[1 - member, :, at].astype(jnp.bfloat16)
                core_copy(part).start()
                xout[micro, member, :, at] = (
                    xin[micro, member, :, at].astype(jnp.float32) + pair_sum[member, :, at]
                ).astype(jnp.bfloat16)
            if step >= 2:
                part = step - 2
                at = columns(part)
                core_copy(part).wait()
                xout[micro, 1 - member, :, at] = (
                    xin[micro, 1 - member, :, at].astype(jnp.float32)
                    + r_core[:, at].astype(jnp.float32)
                ).astype(jnp.bfloat16)

                @pl.when(section < last)
                def _():
                    relay_copy(micro, part).start()

        @pl.when(jnp.logical_and(section == last, micro < last))
        def _():
            final_copy(micro).start()

        for part in range(n_part):
            for rel in range(1, n_chip):
                reduce_copy(part, rel).wait_send()
        return unused

    lax.fori_loop(0, micro_count, one_micro, 0)

    @pl.when(section < last)
    def _():
        for micro in range(micro_count):
            for part in range(n_part):
                relay_copy(micro, part).wait_send()
        final_copy(0).wait_recv()
        for side in range(2):
            out_ref[0, :, pl.ds(side * half, half)] = fin[side]

    @pl.when(section == last)
    def _():
        for micro in range(micro_count - 1):
            final_copy(micro).wait_send()
        for side in range(2):
            out_ref[0, :, pl.ds(side * half, half)] = xout[micro_count - 1, side]


def on_device(inputs, norm_gain, router_weight, gate_weight, up_weight, down_weight, routing):
    n_pp, n_ep = lax.axis_size("pp"), lax.axis_size("ep")
    micro_count, rows, width = inputs.shape
    experts = router_weight.shape[2]
    hid = gate_weight.shape[2]
    half = width // 2
    n_part = len(cut(half))
    n_chip = n_ep // 2
    router_rows = router_weight[0].T.astype(jnp.float32)
    bf16, f32 = jnp.bfloat16, jnp.float32
    dma = pltpu.SemaphoreType.DMA
    any_spec = pl.BlockSpec(memory_space=pl.ANY)
    vmem_spec = pl.BlockSpec(memory_space=pltpu.VMEM)
    return pl.pallas_call(
        functools.partial(kernel, n_pp, n_ep, experts),
        out_shape=jax.ShapeDtypeStruct((1, rows, width), bf16),
        in_specs=[any_spec, vmem_spec, vmem_spec, any_spec, any_spec, any_spec, vmem_spec],
        out_specs=vmem_spec,
        scratch_shapes=[
            pltpu.VMEM((micro_count, 2, rows, half), bf16),
            pltpu.VMEM((micro_count, 2, rows, half), bf16),
            pltpu.VMEM((2, rows, half), bf16),
            pltpu.VMEM((2, n_ep, rows, half), bf16),
            pltpu.VMEM((n_ep, rows, 128), f32),
            pltpu.VMEM((width, hid), bf16),
            pltpu.VMEM((width, hid), bf16),
            pltpu.VMEM((2 * hid, half), bf16),
            pltpu.VMEM((n_ep * rows, hid), f32),
            pltpu.VMEM((n_ep * rows, hid), f32),
            pltpu.VMEM((n_ep * rows, 128), f32),
            pltpu.VMEM((n_ep * rows, hid), bf16),
            pltpu.VMEM((n_ep * rows, hid), bf16),
            pltpu.VMEM((n_chip, 2 * rows, half), f32),
            pltpu.VMEM((2, rows, half), f32),
            pltpu.VMEM((n_chip - 1, 2 * rows, half), bf16),
            pltpu.VMEM((n_chip - 1, 2 * rows, half), bf16),
            pltpu.VMEM((rows, half), bf16),
            pltpu.VMEM((rows, half), bf16),
            dma((2,)), dma((3,)), dma((n_part + 1, n_ep)), dma((n_part + 1, n_ep)), dma, dma,
            dma((n_part, n_chip)), dma((n_part, n_chip)), dma((n_part,)), dma((n_part,)),
            dma((micro_count, n_part)), dma((micro_count, n_part)), dma((micro_count,)), dma,
        ],
        compiler_params=pltpu.CompilerParams(
            collective_id=0, has_side_effects=True, vmem_limit_bytes=60 * 1024 * 1024
        ),
    )(inputs, norm_gain, router_rows, gate_weight, up_weight, down_weight, routing[0])


def solution(mesh):
    return jax.shard_map(
        on_device,
        mesh=mesh,
        in_specs=(
            P(None, "ep", None),
            P("pp", None),
            P("pp", None, None),
            P("pp", None, "ep"),
            P("pp", None, "ep"),
            P("pp", None, "ep"),
            P("pp", None, "ep", None),
        ),
        out_specs=P("pp", "ep", None),
        check_vma=False,
    )
```

```python
import functools

import jax
import jax.numpy as jnp
from jax import lax
from jax.experimental import pallas as pl
from jax.experimental.pallas import tpu as pltpu
from jax.sharding import PartitionSpec as P

routed_scale = 2.5
norm_epsilon = 1e-06


def kernel(
    n_pp, n_ep, experts,
    inputs_ref, gain_ref, router_ref, gate_hbm, up_hbm, down_hbm, routing_ref,
    out_ref,
    xin, xout, fin, tokens, mixes, wg, wu, wd, acc_g, acc_u, hid_own, hid_par, partial, pair_sum,
    s_buf, r_buf, s_core, r_core,
    load_sem, weight_sem, tok_send, tok_recv, hid_send, hid_recv, red_send, red_recv,
    core_send, core_recv, x_send, x_recv, fin_send, fin_recv,
):
    section = lax.axis_index("pp")
    me = lax.axis_index("ep")
    member, chip = me % 2, me // 2
    last = n_pp - 1
    bits = n_ep.bit_length() - 1
    micro_count, rows, width = xin.shape
    half = width // 2
    quarter = half // 2
    n_chip = n_ep // 2
    all_rows = n_ep * rows
    hid = wg.shape[1]

    def at_bit(b):
        return me + (1 << b) - 2 * (1 << b) * ((me // (1 << b)) % 2)

    def flip(value, mask):
        for b in range(bits):
            if mask >> b & 1:
                value = value + (1 << b) - 2 * (1 << b) * ((value // (1 << b)) % 2)
        return value

    copies = [
        pltpu.make_async_copy(gate_hbm.at[0], wg, weight_sem.at[0]),
        pltpu.make_async_copy(up_hbm.at[0], wu, weight_sem.at[1]),
        pltpu.make_async_copy(down_hbm.at[0], wd, weight_sem.at[2]),
    ]
    load = pltpu.make_async_copy(inputs_ref, xin, load_sem)

    @pl.when(section == 0)
    def _():
        load.start()

    for copy in copies:
        copy.start()

    barrier = pltpu.get_barrier_semaphore()
    for b in range(bits):
        pl.semaphore_signal(
            barrier, inc=1, device_id={"ep": at_bit(b)}, device_id_type=pl.DeviceIdType.MESH
        )
    for step in range(1, n_pp):
        pl.semaphore_signal(
            barrier, inc=1, device_id={"pp": (section + step) % n_pp},
            device_id_type=pl.DeviceIdType.MESH,
        )
    pl.semaphore_wait(barrier, bits + n_pp - 1)

    @pl.when(section == 0)
    def _():
        load.wait()

    chip_bits = list(range(1, bits))
    gather_orders = [chip_bits + [0], chip_bits[::-1] + [0], chip_bits + [0]]

    def token_copy(stream, rel):
        order = gather_orders[stream]
        hop = [b for b in order if rel >> b & 1][-1]
        source = flip(me, rel ^ (1 << hop))
        ref = mixes.at[source] if stream == 2 else tokens.at[stream, source]
        return pltpu.make_async_remote_copy(
            src_ref=ref, dst_ref=ref,
            send_sem=tok_send.at[stream, rel], recv_sem=tok_recv.at[stream, rel],
            device_id={"ep": at_bit(hop)}, device_id_type=pl.DeviceIdType.MESH,
        )

    def token_arrival(stream, rel):
        ref = mixes.at[flip(me, rel)] if stream == 2 else tokens.at[stream, flip(me, rel)]
        pltpu.make_async_remote_copy(
            src_ref=ref, dst_ref=ref,
            send_sem=tok_send.at[stream, rel], recv_sem=tok_recv.at[stream, rel],
            device_id={"ep": at_bit(0)}, device_id_type=pl.DeviceIdType.MESH,
        ).wait_recv()

    def onward(stream, rel):
        order = gather_orders[stream]
        start = max([order.index(b) for b in range(bits) if rel >> b & 1], default=-1) + 1
        return [rel | 1 << b for b in order[start:]]

    reduce_orders = [list(range(bits - 1)), list(range(bits - 1))[::-1]]

    def first_place(part, rel):
        return min(i for i, b in enumerate(reduce_orders[part]) if rel >> b & 1)

    def reduce_copy(part, rel):
        hop = reduce_orders[part][first_place(part, rel)]
        return pltpu.make_async_remote_copy(
            src_ref=s_buf.at[part, rel - 1], dst_ref=r_buf.at[part, rel - 1],
            send_sem=red_send.at[part, rel], recv_sem=red_recv.at[part, rel],
            device_id={"ep": at_bit(hop + 1)}, device_id_type=pl.DeviceIdType.MESH,
        )

    def reduced(part, rel):
        place = len(reduce_orders[part]) if rel == 0 else first_place(part, rel)
        value = partial[part, flip(me, rel << 1) // 2]
        for b in reduce_orders[part][:place]:
            reduce_copy(part, rel | 1 << b).wait_recv()
            value = value + r_buf[part, (rel | 1 << b) - 1].astype(jnp.float32)
        return value

    def in_phase(part, place):
        found = [q for q in range(1, n_chip) if first_place(part, q) == place]
        return sorted(found, key=lambda q: -bin(q).count("1"))

    hid_copy = pltpu.make_async_remote_copy(
        src_ref=hid_own, dst_ref=hid_par, send_sem=hid_send, recv_sem=hid_recv,
        device_id={"ep": at_bit(0)}, device_id_type=pl.DeviceIdType.MESH,
    )

    def core_copy(part):
        return pltpu.make_async_remote_copy(
            src_ref=s_core.at[part], dst_ref=r_core.at[part],
            send_sem=core_send.at[part], recv_sem=core_recv.at[part],
            device_id={"ep": at_bit(0)}, device_id_type=pl.DeviceIdType.MESH,
        )

    def relay_copy(micro):
        return pltpu.make_async_remote_copy(
            src_ref=xout.at[micro], dst_ref=xin.at[micro],
            send_sem=x_send.at[micro], recv_sem=x_recv.at[micro],
            device_id={"pp": (section + 1) % n_pp}, device_id_type=pl.DeviceIdType.MESH,
        )

    def final_copy(micro):
        return pltpu.make_async_remote_copy(
            src_ref=xout.at[micro], dst_ref=fin,
            send_sem=fin_send.at[micro], recv_sem=fin_recv,
            device_id={"pp": micro}, device_id_type=pl.DeviceIdType.MESH,
        )

    def one_micro(micro, unused):
        @pl.when(section > 0)
        def _():
            relay_copy(micro).wait_recv()

        current = xin[micro].astype(jnp.float32)
        mean_square = jnp.mean(current * current, axis=1, keepdims=True)
        normed = (current * lax.rsqrt(mean_square + norm_epsilon) * gain_ref[...]).astype(
            jnp.bfloat16
        )
        tokens[0, me] = normed[:, :half]
        tokens[1, me] = normed[:, half:]
        own = [onward(stream, 0) for stream in range(2)]
        for place in range(bits):
            for stream in range(2):
                token_copy(stream, own[stream][place]).start()

        normed32 = normed.astype(jnp.float32)
        routes = routing_ref[micro]
        top = routes.shape[1]
        picked = [jnp.zeros((rows, 1), jnp.float32) for k in range(top)]
        for e in range(experts):
            logit = jnp.sum(normed32 * router_ref[e : e + 1, :], axis=1, keepdims=True)
            score = jax.nn.sigmoid(logit)
            for k in range(top):
                picked[k] = picked[k] + jnp.where(routes[:, k : k + 1] == e, score, 0.0)
        total = functools.reduce(lambda a, b: a + b, picked)
        lanes = lax.broadcasted_iota(jnp.int32, (rows, 128), 1)
        mix = jnp.zeros((rows, 128), jnp.float32)
        for k in range(top):
            share = routed_scale * picked[k] / total
            mix = mix + jnp.where(lanes == routes[:, k : k + 1], share, 0.0)
        mixes[me] = mix
        for rel in onward(2, 0):
            token_copy(2, rel).start()

        order = sorted(range(1, n_ep), key=lambda r: (bin(r >> 1).count("1"), r & 1))
        for rel in order:
            for stream in range(3):
                token_arrival(stream, rel)
                for later in onward(stream, rel):
                    token_copy(stream, later).start()

        @pl.when(micro == 0)
        def _():
            copies[0].wait()
            copies[1].wait()

        acc_g[...] = jnp.zeros_like(acc_g)
        acc_u[...] = jnp.zeros_like(acc_u)
        depth = half // 2
        for stream in range(2):

            def project(i, carry, stream=stream):
                at = pl.multiple_of(i * depth, depth)
                block = tokens[stream, :, :, pl.ds(at, depth)].reshape(all_rows, depth)
                where = pl.ds(pl.multiple_of(stream * half + at, depth), depth)
                acc_g[...] += jnp.dot(block, wg[where, :], preferred_element_type=jnp.float32)
                acc_u[...] += jnp.dot(block, wu[where, :], preferred_element_type=jnp.float32)
                return carry

            lax.fori_loop(0, half // depth, project, 0)
        gate_proj = acc_g[...]
        hid_own[...] = (gate_proj / (1.0 + jnp.exp(-gate_proj)) * acc_u[...]).astype(jnp.bfloat16)
        hid_copy.start()
        for rel in range(1, n_ep):
            for stream in range(3):
                token_copy(stream, rel).wait_send()

        @pl.when(micro == 0)
        def _():
            copies[2].wait()

        lane3 = lax.broadcasted_iota(jnp.int32, (n_ep, rows, 128), 2)
        mix_all = jnp.sum(
            jnp.where(lane3 == chip, mixes[...], 0.0), axis=2, keepdims=True
        ).reshape(all_rows, 1)
        hid_copy.wait()

        tile = quarter
        own_rows = pl.ds(pl.multiple_of(member * hid, hid), hid)
        par_rows = pl.ds(pl.multiple_of((1 - member) * hid, hid), hid)
        for part in range(2):

            def down(i, carry, part=part):
                at = pl.ds(pl.multiple_of(part * quarter + i * tile, tile), tile)
                value = jnp.dot(hid_own[...], wd[own_rows, at], preferred_element_type=jnp.float32)
                value += jnp.dot(hid_par[...], wd[par_rows, at], preferred_element_type=jnp.float32)
                value = value * mix_all
                to = pl.ds(pl.multiple_of(i * tile, tile), tile)
                partial[part, :, :, to] = value.reshape(n_chip, 2 * rows, tile)
                return carry

            lax.fori_loop(0, quarter // tile, down, 0)
            for rel in in_phase(part, 0):
                s_buf[part, rel - 1] = reduced(part, rel).astype(jnp.bfloat16)
                reduce_copy(part, rel).start()
        for place in range(1, bits - 1):
            for part in range(2):
                for rel in in_phase(part, place):
                    s_buf[part, rel - 1] = reduced(part, rel).astype(jnp.bfloat16)
                    reduce_copy(part, rel).start()
        for part in range(2):
            pair_sum[part] = reduced(part, 0).reshape(2, rows, quarter)
            s_core[part] = pair_sum[part, 1 - member].astype(jnp.bfloat16)
            core_copy(part).start()
        for part in range(2):
            at = pl.ds(pl.multiple_of(member * half + part * quarter, 128), quarter)
            xout[micro, :, at] = (
                xin[micro, :, at].astype(jnp.float32) + pair_sum[part, member]
            ).astype(jnp.bfloat16)
        for part in range(2):
            core_copy(part).wait()
            at = pl.ds(pl.multiple_of((1 - member) * half + part * quarter, 128), quarter)
            xout[micro, :, at] = (
                xin[micro, :, at].astype(jnp.float32) + r_core[part].astype(jnp.float32)
            ).astype(jnp.bfloat16)

        @pl.when(section < last)
        def _():
            relay_copy(micro).start()

        @pl.when(jnp.logical_and(section == last, micro < last))
        def _():
            final_copy(micro).start()

        for part in range(2):
            for rel in range(1, n_chip):
                reduce_copy(part, rel).wait_send()
        return unused

    lax.fori_loop(0, micro_count, one_micro, 0)

    @pl.when(section < last)
    def _():
        for micro in range(micro_count):
            relay_copy(micro).wait_send()
        final_copy(0).wait_recv()
        out_ref[0] = fin[...]

    @pl.when(section == last)
    def _():
        for micro in range(micro_count - 1):
            final_copy(micro).wait_send()
        out_ref[0] = xout[micro_count - 1]


def on_device(inputs, norm_gain, router_weight, gate_weight, up_weight, down_weight, routing):
    n_pp, n_ep = lax.axis_size("pp"), lax.axis_size("ep")
    micro_count, rows, width = inputs.shape
    experts = router_weight.shape[2]
    hid = gate_weight.shape[2]
    half = width // 2
    quarter = half // 2
    n_chip = n_ep // 2
    router_rows = router_weight[0].T.astype(jnp.float32)
    bf16, f32 = jnp.bfloat16, jnp.float32
    dma = pltpu.SemaphoreType.DMA
    any_spec = pl.BlockSpec(memory_space=pl.ANY)
    vmem_spec = pl.BlockSpec(memory_space=pltpu.VMEM)
    return pl.pallas_call(
        functools.partial(kernel, n_pp, n_ep, experts),
        out_shape=jax.ShapeDtypeStruct((1, rows, width), bf16),
        in_specs=[any_spec, vmem_spec, vmem_spec, any_spec, any_spec, any_spec, vmem_spec],
        out_specs=vmem_spec,
        scratch_shapes=[
            pltpu.VMEM((micro_count, rows, width), bf16),
            pltpu.VMEM((micro_count, rows, width), bf16),
            pltpu.VMEM((rows, width), bf16),
            pltpu.VMEM((2, n_ep, rows, half), bf16),
            pltpu.VMEM((n_ep, rows, 128), f32),
            pltpu.VMEM((width, hid), bf16),
            pltpu.VMEM((width, hid), bf16),
            pltpu.VMEM((2 * hid, half), bf16),
            pltpu.VMEM((n_ep * rows, hid), f32),
            pltpu.VMEM((n_ep * rows, hid), f32),
            pltpu.VMEM((n_ep * rows, hid), bf16),
            pltpu.VMEM((n_ep * rows, hid), bf16),
            pltpu.VMEM((2, n_chip, 2 * rows, quarter), f32),
            pltpu.VMEM((2, 2, rows, quarter), f32),
            pltpu.VMEM((2, n_chip - 1, 2 * rows, quarter), bf16),
            pltpu.VMEM((2, n_chip - 1, 2 * rows, quarter), bf16),
            pltpu.VMEM((2, rows, quarter), bf16),
            pltpu.VMEM((2, rows, quarter), bf16),
            dma, dma((3,)), dma((3, n_ep)), dma((3, n_ep)), dma, dma,
            dma((2, n_chip)), dma((2, n_chip)), dma((2,)), dma((2,)),
            dma((micro_count,)), dma((micro_count,)), dma((micro_count,)), dma,
        ],
        compiler_params=pltpu.CompilerParams(
            collective_id=0, has_side_effects=True, vmem_limit_bytes=60 * 1024 * 1024
        ),
    )(inputs, norm_gain, router_rows, gate_weight, up_weight, down_weight, routing[0])


def solution(mesh):
    return jax.shard_map(
        on_device,
        mesh=mesh,
        in_specs=(
            P(None, "ep", None),
            P("pp", None),
            P("pp", None, None),
            P("pp", None, "ep"),
            P("pp", None, "ep"),
            P("pp", None, "ep"),
            P("pp", None, "ep", None),
        ),
        out_specs=P("pp", "ep", None),
        check_vma=False,
    )
```
